32 devices in a mesh: scan: 8 (over z, x), col: 4 (over y, core).
Axes of the slice: x: 2, y: 2, z: 4, core: 2. Of those that a mesh axis runs over, the one named last changes fastest.
Arguments:
- object_field: float32 [2, 2048, 1024], P(None, 'scan', 'col'), may hold values from -6 to 6
- amplitudes: bfloat16 [64, 256, 256], P(('scan', 'col')), may hold values from 0.099609375 to 3
- positions: int32 [64, 2], P(('scan', 'col')), may hold values from 0 to 1792, as said below
- frame_count: int32 [32], P(('scan', 'col')), may hold values from 1 to 2, as said below
- coefficients: float32 [64, 4], P(('scan', 'col')), may hold values from -6 to 6
- probe_modes: float32 [4, 2, 256, 256], replicated, may hold values from -6 to 6
Outputs:
- refined_object: float32 [2, 2048, 1024], P(None, 'scan', 'col')
- refined_modes: float32 [4, 2, 256, 256], replicated
- refined_coefficients: float32 [64, 4], P(('scan', 'col'))
The draws below stay inside these ranges and needn't reach their ends.
Inputs may be any that keep to these rules, and one draw needn't show every extreme that they name: `positions`: frame g belongs to the device of index g // 2 along scan+col (scan slowest). Its top-left pixel lies in that device's block of 256 x 256 pixels, and its 256 x 256 patch lies inside the object. Entry d counts the live frames of the device of index d along scan+col: its first frame_count[d] slots are live, the rest are ignored. Some device has 2.
All inputs are finite; a program needn't handle non-finite values.
Results may differ from the reference program's by a relative error of at most 0.0058.
Values sent between devices are 32-bit elements; how exact they have to be, the bound alone decides.
A program may use at most 128 MiB of HBM per device.

```python
import math
import jax
import jax.numpy as jnp
from jax import lax

FS = 256
MODES = 4
ITERS = 2
F_DEV = 2
BH = 256
BW = 256
FRAMES = 64
OH = 2048
OW = 1024
N_SCAN = 8
N_COL = 4


def draw_positions(key, part):
    devices = N_SCAN * N_COL
    frames = F_DEV * devices
    slot_index = jnp.arange(frames, dtype=jnp.int32)
    device = slot_index // F_DEV
    scan_index = device // N_COL
    col_index = device % N_COL
    row_key, col_key = jax.random.split(jax.random.fold_in(key, 11))
    row_limit = jnp.where(scan_index < N_SCAN - 1, BH, BH - FS + 1).astype(jnp.int32)
    col_limit = jnp.where(col_index < N_COL - 1, BW, BW - FS + 1).astype(jnp.int32)
    row_offset = jax.random.randint(row_key, (frames,), 0, row_limit, dtype=jnp.int32)
    col_offset = jax.random.randint(col_key, (frames,), 0, col_limit, dtype=jnp.int32)
    return jnp.stack([scan_index * BH + row_offset, col_index * BW + col_offset], 1).astype(jnp.int32)


def draw_frame_count(key, part):
    devices = N_SCAN * N_COL
    pick_key, count_key = jax.random.split(jax.random.fold_in(key, 23))
    raw_draw = jax.random.randint(count_key, (devices,), 0, F_DEV, dtype=jnp.int32)
    counts = jnp.maximum(1, raw_draw * raw_draw // F_DEV)
    chosen = jax.random.randint(pick_key, (), 0, devices, dtype=jnp.int32)
    return jnp.where(jnp.arange(devices, dtype=jnp.int32) == chosen, F_DEV, counts).astype(jnp.int32)


def block_scale(stream_key, extent, shards, least, top_value):
    gain = 1.0
    for position, shards_of in shards:
        draws = jax.random.uniform(jax.random.fold_in(jax.random.fold_in(stream_key, 6), position), (shards_of,), jnp.float32, least / len(shards), top_value / len(shards))
        gain = gain * jnp.repeat(jnp.exp(draws), extent[position] // shards_of).reshape((-1,) + (1,) * (len(extent) - 1 - position))
    return gain


def scatter_about(stream_key, shape, deviation, most, pieces=(), kind=jnp.bfloat16):
    drawn = jax.random.normal(stream_key, shape, jnp.float32) * deviation
    if len(pieces) > 0:
        drawn = block_scale(stream_key, shape, pieces, -0.22, 0.18) * drawn
    return jnp.clip(drawn, min=-most, max=most).astype(kind)


def setup_inputs(seed: int = 0) -> dict:
    splits = jax.random.split(jax.random.key(seed), 7)
    object_field = scatter_about(splits[0], (2, OH, OW), 1.0, 6.0, ((1, 8), (2, 4)), jnp.float32)
    amplitudes = jnp.clip(jnp.exp(math.log(3.0) - 3.4051113 * jax.random.uniform(splits[1], (FRAMES, FS, FS), jnp.float32) ** block_scale(splits[1], (FRAMES, FS, FS), ((0, 32),), -0.2, 0.2)), 0.099609375, 3.0).astype(jnp.bfloat16)
    positions = draw_positions(jax.random.fold_in(splits[6], 71), 0)
    frame_count = draw_frame_count(jax.random.fold_in(splits[6], 71), 0)
    coefficients = scatter_about(splits[4], (FRAMES, MODES), 1.0, 6.0, ((0, 32),), jnp.float32)
    probe_modes = scatter_about(splits[5], (MODES, 2, FS, FS), 1.0, 6.0, (), jnp.float32)
    return dict(object_field=object_field, amplitudes=amplitudes, positions=positions, frame_count=frame_count, coefficients=coefficients, probe_modes=probe_modes)


highest = lax.Precision.HIGHEST

def make_tables(length):
    indices = jnp.arange(length, dtype=jnp.int32)
    phases = indices[:, None] * indices[None, :] % length
    angles = phases.astype(jnp.float32) * (2.0 * math.pi / length)
    factor = 1.0 / math.sqrt(length)
    cosine = jnp.cos(angles) * factor
    sine_table = jnp.sin(angles) * factor
    rows_table = jnp.concatenate([jnp.concatenate([cosine, sine_table], 1), jnp.concatenate([-sine_table, cosine], 1)], 0)
    cols_table = jnp.concatenate([jnp.concatenate([cosine, -sine_table], 1), jnp.concatenate([sine_table, cosine], 1)], 0)
    return (rows_table.astype(jnp.bfloat16), cols_table.astype(jnp.bfloat16))

def apply_transform(real_part, imag_part, first_table, second_table):
    length = real_part.shape[0]
    stacked = jnp.concatenate([real_part, imag_part], 0)
    halfway = jnp.dot(first_table, stacked, preferred_element_type=jnp.float32).astype(jnp.bfloat16)
    beside = jnp.concatenate([halfway[:length], halfway[length:]], 1)
    result = jnp.dot(beside, second_table, preferred_element_type=jnp.float32)
    return (result[:, :length], result[:, length:])

def frame_update(object_patch, probe_field, amplitude, rows_table, cols_table):
    probe_real = probe_field[0]
    probe_imag = probe_field[1]
    object_real = object_patch[0]
    object_imag = object_patch[1]
    exit_real = probe_real * object_real - probe_imag * object_imag
    exit_imag = probe_real * object_imag + probe_imag * object_real
    far_real, far_imag = apply_transform(exit_real.astype(jnp.bfloat16), exit_imag.astype(jnp.bfloat16), rows_table, cols_table)
    magnitude = jnp.sqrt(far_real * far_real + far_imag * far_imag)
    factor = amplitude.astype(jnp.float32) / jnp.maximum(magnitude, 0.5)
    new_real, new_imag = apply_transform((far_real * factor).astype(jnp.bfloat16), (far_imag * factor).astype(jnp.bfloat16), cols_table, rows_table)
    diff_real = new_real - exit_real
    diff_imag = new_imag - exit_imag
    update = jnp.stack([probe_real * diff_real + probe_imag * diff_imag, probe_real * diff_imag - probe_imag * diff_real, probe_real * probe_real + probe_imag * probe_imag])
    probe_step = jnp.stack([object_real * diff_real + object_imag * diff_imag, object_real * diff_imag - object_imag * diff_real])
    return (update, probe_step)

def gram_parts(flat_modes):
    real_plane = flat_modes[:, 0]
    imag_plane = flat_modes[:, 1]
    gram_real = jnp.dot(real_plane, real_plane.T, precision=highest, preferred_element_type=jnp.float32) + jnp.dot(imag_plane, imag_plane.T, precision=highest, preferred_element_type=jnp.float32)
    gram_imag = jnp.dot(real_plane, imag_plane.T, precision=highest, preferred_element_type=jnp.float32) - jnp.dot(imag_plane, real_plane.T, precision=highest, preferred_element_type=jnp.float32)
    return (gram_real, gram_imag)

def orthonormal(flat_modes, gram_real, gram_imag):
    mode_count = flat_modes.shape[0]
    upper_real = [[None] * mode_count for other in range(mode_count)]
    upper_imag = [[None] * mode_count for other in range(mode_count)]
    for right_index in range(mode_count):
        for left_index in range(right_index):
            sum_real = gram_real[left_index, right_index]
            sum_imag = gram_imag[left_index, right_index]
            for inner_index in range(left_index):
                first_real = upper_real[inner_index][left_index]
                first_imag = upper_imag[inner_index][left_index]
                second_real = upper_real[inner_index][right_index]
                second_imag = upper_imag[inner_index][right_index]
                sum_real = sum_real - (first_real * second_real + first_imag * second_imag)
                sum_imag = sum_imag - (first_real * second_imag - first_imag * second_real)
            upper_real[left_index][right_index] = sum_real / upper_real[left_index][left_index]
            upper_imag[left_index][right_index] = sum_imag / upper_real[left_index][left_index]
        diagonal = gram_real[right_index, right_index]
        for inner_index in range(right_index):
            entry_real = upper_real[inner_index][right_index]
            entry_imag = upper_imag[inner_index][right_index]
            diagonal = diagonal - (entry_real * entry_real + entry_imag * entry_imag)
        upper_real[right_index][right_index] = jnp.sqrt(diagonal)
    columns = []
    for right_index in range(mode_count):
        vector_real = flat_modes[right_index, 0]
        vector_imag = flat_modes[right_index, 1]
        for left_index in range(right_index):
            basis_real, basis_imag = columns[left_index]
            entry_real = upper_real[left_index][right_index]
            entry_imag = upper_imag[left_index][right_index]
            vector_real = vector_real - (entry_real * basis_real - entry_imag * basis_imag)
            vector_imag = vector_imag - (entry_real * basis_imag + entry_imag * basis_real)
        pivot = upper_real[right_index][right_index]
        columns.append((vector_real / pivot, vector_imag / pivot))
    return jnp.stack([jnp.stack([pair[0], pair[1]]) for pair in columns])

def reference(object_field, amplitudes, positions, frame_count, coefficients, probe_modes):
    frames = amplitudes.shape[0]
    length = amplitudes.shape[1]
    mode_count = probe_modes.shape[0]
    pixels = length * length
    root_total = math.sqrt(frames)
    rows_table, cols_table = make_tables(length)
    slot_index = jnp.arange(frames, dtype=jnp.int32)
    owner = (slot_index // F_DEV).astype(jnp.int32)
    live_mask = slot_index % F_DEV < frame_count[owner]
    anchor = jnp.zeros((), jnp.int32)
    for iteration in range(ITERS):
        current_object = object_field
        current_modes = probe_modes

        def visit(state, item):
            amplitude, offset, weights, alive = item

            def work(inner):
                totals, mode_terms = inner
                object_patch = lax.dynamic_slice(current_object, (anchor, offset[0], offset[1]), (2, length, length))
                probe_field = jnp.tensordot(weights, current_modes, axes=1, precision=highest)
                update, probe_step = frame_update(object_patch, probe_field, amplitude, rows_table, cols_table)
                window = lax.dynamic_slice(totals, (anchor, offset[0], offset[1]), (3, length, length))
                totals = lax.dynamic_update_slice(totals, window + update, (anchor, offset[0], offset[1]))
                mode_terms = mode_terms + weights[:, None, None, None] * probe_step[None]
                return ((totals, mode_terms), probe_step)

            def skip(inner):
                return (inner, jnp.zeros((2, length, length), jnp.float32))
            return lax.cond(alive, work, skip, state)
        initial = (jnp.zeros((3,) + object_field.shape[1:], jnp.float32), jnp.zeros((mode_count, 2, length, length), jnp.float32))
        (totals, mode_terms), stashed = lax.scan(visit, initial, (amplitudes, positions, coefficients, live_mask))
        object_field = object_field + totals[:2] / (totals[2] + 1.0)
        raised = (probe_modes + mode_terms / root_total).reshape(mode_count, 2, pixels)
        gram_real, gram_imag = gram_parts(raised)
        orthogonal = orthonormal(raised, gram_real / pixels, gram_imag / pixels)
        ortho_flat = orthogonal.reshape(mode_count, 2 * pixels)
        mixing = jnp.dot(probe_modes.reshape(mode_count, 2 * pixels), ortho_flat.T, precision=highest, preferred_element_type=jnp.float32) / pixels
        projected = jnp.dot(stashed.reshape(frames, 2 * pixels), ortho_flat.T, precision=highest, preferred_element_type=jnp.float32) / pixels
        refit = jnp.dot(coefficients, mixing, precision=highest, preferred_element_type=jnp.float32) + 0.5 * projected
        coefficients = jnp.where(live_mask[:, None], refit, coefficients)
        probe_modes = orthogonal.reshape(mode_count, 2, length, length)
    return (object_field, probe_modes, coefficients)
```

```python
import math

import jax
import jax.numpy as jnp
from jax import lax
from jax.experimental import pallas as pl
from jax.experimental.pallas import tpu as pltpu
from jax.sharding import PartitionSpec as P

ITERS = 2

VMEM = pl.BlockSpec(memory_space=pltpu.VMEM)
SMEM = pl.BlockSpec(memory_space=pltpu.SMEM)


def from_behind(shard, axis, by):
    size = lax.axis_size(axis)
    pairs = [(i, i + by) for i in range(size) if 0 <= i + by < size]
    return lax.ppermute(shard, axis, pairs)


def make_tables(length):
    indices = jnp.arange(length, dtype=jnp.int32)
    phases = indices[:, None] * indices[None, :] % length
    angles = phases.astype(jnp.float32) * (2.0 * math.pi / length)
    factor = 1.0 / math.sqrt(length)
    cosine = jnp.cos(angles) * factor
    sine_table = jnp.sin(angles) * factor
    rows_table = jnp.concatenate(
        [jnp.concatenate([cosine, sine_table], 1), jnp.concatenate([-sine_table, cosine], 1)], 0
    )
    cols_table = jnp.concatenate(
        [jnp.concatenate([cosine, -sine_table], 1), jnp.concatenate([sine_table, cosine], 1)], 0
    )
    return (rows_table.astype(jnp.bfloat16), cols_table.astype(jnp.bfloat16))


def apply_transform(stacked, first_table, second_table):
    length = stacked.shape[1]
    halfway = jnp.dot(first_table, stacked, preferred_element_type=jnp.float32).astype(jnp.bfloat16)
    beside = jnp.concatenate([halfway[:length], halfway[length:]], 1)
    return jnp.dot(beside, second_table, preferred_element_type=jnp.float32)


def frames_kernel(
    count, offsets, weights, home, beyond, lower, corner, amplitudes, modes, rows_table, cols_table,
    totals, mode_terms, stashed, wide,
):
    length = amplitudes.shape[1]
    block_height, block_width = home.shape[1:]
    mode_count = modes.shape[0] // 2
    wide[:, :block_height, :block_width] = home[...]
    wide[:, :block_height, block_width:] = beyond[...]
    wide[:, block_height:, :block_width] = lower[...]
    wide[:, block_height:, block_width:] = corner[...]
    totals[...] = jnp.zeros_like(totals)
    mode_terms[...] = jnp.zeros_like(mode_terms)
    stashed[...] = jnp.zeros_like(stashed)
    full_width = block_width + length

    def visit(slot, carry):
        row, col = offsets[slot, 0], offsets[slot, 1]
        start = pl.multiple_of(row // 8 * 8, 8)
        rest = row - start
        rows = pl.ds(start, length + 8)

        def cut(plane):
            band = wide[plane, rows, :]
            band = pltpu.roll(band, lax.rem(full_width - col, full_width), 1)[:, :length]
            return pltpu.roll(band, lax.rem(length + 8 - rest, length + 8), 0)[:length]

        def place(plane, piece):
            band = jnp.concatenate([piece, jnp.zeros((8, length), jnp.float32)], 0)
            band = pltpu.roll(band, rest, 0)
            band = jnp.concatenate([band, jnp.zeros((length + 8, block_width), jnp.float32)], 1)
            totals[plane, rows, :] += pltpu.roll(band, col, 1)

        object_real = cut(0)
        object_imag = cut(1)
        probe_real = weights[slot, 0] * modes[0]
        probe_imag = weights[slot, 0] * modes[1]
        for k in range(1, mode_count):
            probe_real += weights[slot, k] * modes[2 * k]
            probe_imag += weights[slot, k] * modes[2 * k + 1]
        place(2, probe_real * probe_real + probe_imag * probe_imag)
        exit_real = probe_real * object_real - probe_imag * object_imag
        exit_imag = probe_real * object_imag + probe_imag * object_real
        stacked = jnp.concatenate([exit_real, exit_imag], 0).astype(jnp.bfloat16)
        far = apply_transform(stacked, rows_table[...], cols_table[...])
        far_real, far_imag = far[:, :length], far[:, length:]
        magnitude = jnp.sqrt(far_real * far_real + far_imag * far_imag)
        factor = amplitudes[slot].astype(jnp.float32) / jnp.maximum(magnitude, 0.5)
        scaled = jnp.concatenate([far_real * factor, far_imag * factor], 0).astype(jnp.bfloat16)
        back = apply_transform(scaled, cols_table[...], rows_table[...])
        diff_real = back[:, :length] - exit_real
        diff_imag = back[:, length:] - exit_imag
        place(0, probe_real * diff_real + probe_imag * diff_imag)
        place(1, probe_real * diff_imag - probe_imag * diff_real)
        step_real = object_real * diff_real + object_imag * diff_imag
        step_imag = object_real * diff_imag - object_imag * diff_real
        stashed[slot, 0] = step_real
        stashed[slot, 1] = step_imag
        for k in range(mode_count):
            mode_terms[2 * k] += weights[slot, k] * step_real
            mode_terms[2 * k + 1] += weights[slot, k] * step_imag
        return carry

    lax.fori_loop(0, count[0], visit, 0)


def refit_kernel(root_total, count, weights, summed, modes, stashed, new_modes, new_weights, lifted):
    planes, length = modes.shape[:2]
    mode_count = planes // 2
    frames = stashed.shape[0]
    pixels = float(length * length)
    height = 8
    steps = length // height
    pairs = [(i, j) for j in range(mode_count) for i in range(j + 1)]
    strict = [(i, j) for i, j in pairs if i < j]

    def fold(value):
        total = value[:, :128]
        for at in range(128, length, 128):
            total = total + value[:, at:at + 128]
        return total

    def at_rows(step):
        return pl.ds(pl.multiple_of(step * height, height), height)

    def gram_step(step, sums):
        rows = at_rows(step)
        raised = []
        for p in range(planes):
            value = modes[p, rows, :] + summed[p, rows, :] / root_total
            lifted[p, rows, :] = value
            raised.append(value)
        real, imag = raised[0::2], raised[1::2]
        terms = [fold(real[i] * real[j] + imag[i] * imag[j]) for i, j in pairs]
        terms += [fold(real[i] * imag[j] - imag[i] * real[j]) for i, j in strict]
        return tuple(a + b for a, b in zip(sums, terms))

    blank = jnp.zeros((height, 128), jnp.float32)
    sums = lax.fori_loop(0, steps, gram_step, (blank,) * (len(pairs) + len(strict)))

    def whole(value):
        return jnp.sum(jnp.sum(value, 0, keepdims=True), 1, keepdims=True)

    gram_real = {p: whole(s) / pixels for p, s in zip(pairs, sums)}
    gram_imag = {p: whole(s) / pixels for p, s in zip(strict, sums[len(pairs):])}
    upper_real, upper_imag = {}, {}
    for j in range(mode_count):
        for i in range(j):
            sum_real, sum_imag = gram_real[i, j], gram_imag[i, j]
            for k in range(i):
                a, b, c, d = upper_real[k, i], upper_imag[k, i], upper_real[k, j], upper_imag[k, j]
                sum_real = sum_real - (a * c + b * d)
                sum_imag = sum_imag - (a * d - b * c)
            upper_real[i, j] = sum_real / upper_real[i, i]
            upper_imag[i, j] = sum_imag / upper_real[i, i]
        diagonal = gram_real[j, j]
        for k in range(j):
            diagonal = diagonal - (upper_real[k, j] * upper_real[k, j] + upper_imag[k, j] * upper_imag[k, j])
        upper_real[j, j] = jnp.sqrt(diagonal)
    wide = {p: jnp.broadcast_to(v, (height, length)) for p, v in upper_real.items()}
    wide_imag = {p: jnp.broadcast_to(v, (height, length)) for p, v in upper_imag.items()}
    inverse = {j: jnp.broadcast_to(1.0 / upper_real[j, j], (height, length)) for j in range(mode_count)}

    def basis_step(step, carry):
        rows = at_rows(step)
        basis = []
        for j in range(mode_count):
            real, imag = lifted[2 * j, rows, :], lifted[2 * j + 1, rows, :]
            for i in range(j):
                a, b = wide[i, j], wide_imag[i, j]
                c, d = basis[i]
                real = real - (a * c - b * d)
                imag = imag - (a * d + b * c)
            real, imag = real * inverse[j], imag * inverse[j]
            basis.append((real, imag))
            new_modes[2 * j, rows, :] = real
            new_modes[2 * j + 1, rows, :] = imag
        return carry

    lax.fori_loop(0, steps, basis_step, 0)

    def fit_step(step, sums):
        rows = at_rows(step)
        basis = [new_modes[p, rows, :] for p in range(planes)]
        terms = []
        for j in range(mode_count):
            real, imag = modes[2 * j, rows, :], modes[2 * j + 1, rows, :]
            terms += [fold(basis[2 * k] * real + basis[2 * k + 1] * imag) for k in range(mode_count)]
        for g in range(frames):
            real, imag = stashed[g, 0, rows, :], stashed[g, 1, rows, :]
            terms += [fold(basis[2 * k] * real + basis[2 * k + 1] * imag) for k in range(mode_count)]
        return tuple(a + b for a, b in zip(sums, terms))

    sums = lax.fori_loop(0, steps, fit_step, (blank,) * (mode_count * (mode_count + frames)))
    sums = [whole(s) / pixels for s in sums]
    for g in range(frames):
        for k in range(mode_count):
            refit = 0.5 * sums[mode_count * (mode_count + g) + k]
            for j in range(mode_count):
                refit = refit + weights[g, j] * sums[mode_count * j + k]
            kept = jnp.full((1, 1), weights[g, k], jnp.float32)
            new_weights[g:g + 1, k:k + 1] = jnp.where(g < count[0], refit, kept)


def settle(totals, block_height, block_width, length, col_index, col_count):
    arrived = from_behind(totals[:, :block_height, block_width:], "col", 1)
    lowered = from_behind(totals[:, block_height:, :block_width], "scan", 1)
    corner = from_behind(totals[:, block_height:, block_width:], ("scan", "col"), col_count + 1)
    corner = jnp.where(col_index > 0, corner, jnp.zeros_like(corner))
    settled = totals[:, :block_height, :block_width]
    settled = settled.at[:, :, :length].add(arrived)
    settled = settled.at[:, :length, :].add(lowered)
    settled = settled.at[:, :length, :length].add(corner)
    return settled


def shape(*dims):
    return jax.ShapeDtypeStruct(dims, jnp.float32)


def on_device(object_field, amplitudes, positions, frame_count, coefficients, probe_modes):
    frames, length = amplitudes.shape[:2]
    mode_count = probe_modes.shape[0]
    planes = 2 * mode_count
    block_height, block_width = object_field.shape[1:]
    scan_count = lax.axis_size("scan")
    col_count = lax.axis_size("col")
    col_index = lax.axis_index("col")
    block_corner = jnp.stack([lax.axis_index("scan") * block_height, col_index * block_width])
    offsets = positions - block_corner[None, :]
    root_total = math.sqrt(frames * scan_count * col_count)
    rows_table, cols_table = make_tables(length)
    modes = probe_modes.reshape(planes, length, length)
    for iteration in range(ITERS):
        lower_rim = from_behind(object_field, "scan", -1)
        beyond = from_behind(object_field, "col", -1)
        corner = from_behind(object_field, ("scan", "col"), -(col_count + 1))
        totals, mode_terms, stashed = pl.pallas_call(
            frames_kernel,
            name="frames",
            out_shape=(
                shape(3, block_height + length, block_width + length),
                shape(planes, length, length),
                shape(frames, 2, length, length),
            ),
            in_specs=[SMEM] * 3 + [VMEM] * 8,
            out_specs=(VMEM,) * 3,
            scratch_shapes=[pltpu.VMEM((2, block_height + length, block_width + length), jnp.float32)],
            cost_estimate=pl.CostEstimate(flops=2 * 10**9, bytes_accessed=10**7, transcendentals=0),
        )(
            frame_count, offsets, coefficients, object_field, beyond, lower_rim, corner, amplitudes,
            modes, rows_table, cols_table,
        )
        summed = lax.psum(mode_terms, ("scan", "col"))
        settled = settle(totals, block_height, block_width, length, col_index, col_count)
        object_field = object_field + settled[:2] / (settled[2] + 1.0)
        modes, coefficients = pl.pallas_call(
            lambda *refs: refit_kernel(root_total, *refs),
            name="refit",
            out_shape=(shape(planes, length, length), shape(frames, mode_count)),
            in_specs=[SMEM] * 2 + [VMEM] * 3,
            out_specs=(VMEM,) * 2,
            scratch_shapes=[pltpu.VMEM((planes, length, length), jnp.float32)],
        )(frame_count, coefficients, summed, modes, stashed)
    return (object_field, modes.reshape(probe_modes.shape), coefficients)


def solution(mesh):
    placed = (
        P(None, "scan", "col"),
        P(("scan", "col"), None, None),
        P(("scan", "col"), None),
        P(("scan", "col")),
        P(("scan", "col"), None),
        P(),
    )
    return jax.shard_map(
        on_device,
        mesh=mesh,
        in_specs=placed,
        out_specs=(P(None, "scan", "col"), P(), P(("scan", "col"), None)),
        check_vma=False,
    )
```

```python
import functools
import math

import jax
import jax.numpy as jnp
from jax import lax
from jax.experimental import pallas as pl
from jax.experimental.pallas import tpu as pltpu
from jax.sharding import PartitionSpec as P

ITERS = 2

VMEM = pl.BlockSpec(memory_space=pltpu.VMEM)
SMEM = pl.BlockSpec(memory_space=pltpu.SMEM)


def make_tables(length):
    indices = jnp.arange(length, dtype=jnp.int32)
    phases = indices[:, None] * indices[None, :] % length
    angles = phases.astype(jnp.float32) * (2.0 * math.pi / length)
    factor = 1.0 / math.sqrt(length)
    cosine = jnp.cos(angles) * factor
    sine_table = jnp.sin(angles) * factor
    rows_table = jnp.concatenate(
        [jnp.concatenate([cosine, sine_table], 1), jnp.concatenate([-sine_table, cosine], 1)], 0
    )
    cols_table = jnp.concatenate(
        [jnp.concatenate([cosine, -sine_table], 1), jnp.concatenate([sine_table, cosine], 1)], 0
    )
    return (rows_table.astype(jnp.bfloat16), cols_table.astype(jnp.bfloat16))


def apply_transform(stacked, first_table, second_table):
    length = stacked.shape[1]
    halfway = jnp.dot(first_table, stacked, preferred_element_type=jnp.float32).astype(jnp.bfloat16)
    beside = jnp.concatenate([halfway[:length], halfway[length:]], 1)
    return jnp.dot(beside, second_table, preferred_element_type=jnp.float32)


def frames_kernel(
    count, offsets, weights, wide, amplitudes, modes, rows_table, cols_table,
    totals, mode_terms, stashed,
):
    length = amplitudes.shape[1]
    mode_count = modes.shape[0] // 2
    full_width = wide.shape[2]
    block_width = full_width - length
    totals[...] = jnp.zeros_like(totals)
    mode_terms[...] = jnp.zeros_like(mode_terms)
    stashed[...] = jnp.zeros_like(stashed)

    def visit(slot, carry):
        row, col = offsets[slot, 0], offsets[slot, 1]
        start = pl.multiple_of(row // 8 * 8, 8)
        rest = row - start
        rows = pl.ds(start, length + 8)

        def cut(plane):
            band = wide[plane, rows, :]
            band = pltpu.roll(band, lax.rem(full_width - col, full_width), 1)[:, :length]
            return pltpu.roll(band, lax.rem(length + 8 - rest, length + 8), 0)[:length]

        def place(plane, piece):
            band = jnp.concatenate([piece, jnp.zeros((8, length), jnp.float32)], 0)
            band = pltpu.roll(band, rest, 0)
            band = jnp.concatenate([band, jnp.zeros((length + 8, block_width), jnp.float32)], 1)
            totals[plane, rows, :] += pltpu.roll(band, col, 1)

        object_real = cut(0)
        object_imag = cut(1)
        probe_real = weights[slot, 0] * modes[0]
        probe_imag = weights[slot, 0] * modes[1]
        for k in range(1, mode_count):
            probe_real += weights[slot, k] * modes[2 * k]
            probe_imag += weights[slot, k] * modes[2 * k + 1]
        place(2, probe_real * probe_real + probe_imag * probe_imag)
        exit_real = probe_real * object_real - probe_imag * object_imag
        exit_imag = probe_real * object_imag + probe_imag * object_real
        stacked = jnp.concatenate([exit_real, exit_imag], 0).astype(jnp.bfloat16)
        far = apply_transform(stacked, rows_table[...], cols_table[...])
        far_real, far_imag = far[:, :length], far[:, length:]
        magnitude = jnp.sqrt(far_real * far_real + far_imag * far_imag)
        factor = amplitudes[slot].astype(jnp.float32) / jnp.maximum(magnitude, 0.5)
        scaled = jnp.concatenate([far_real * factor, far_imag * factor], 0).astype(jnp.bfloat16)
        back = apply_transform(scaled, cols_table[...], rows_table[...])
        diff_real = back[:, :length] - exit_real
        diff_imag = back[:, length:] - exit_imag
        place(0, probe_real * diff_real + probe_imag * diff_imag)
        place(1, probe_real * diff_imag - probe_imag * diff_real)
        step_real = object_real * diff_real + object_imag * diff_imag
        step_imag = object_real * diff_imag - object_imag * diff_real
        stashed[slot, 0] = step_real
        stashed[slot, 1] = step_imag
        for k in range(mode_count):
            mode_terms[2 * k] += weights[slot, k] * step_real
            mode_terms[2 * k + 1] += weights[slot, k] * step_imag
        return carry

    lax.fori_loop(0, count[0], visit, 0)


def refit_kernel(root_total, count, weights, summed, modes, stashed, new_modes, new_weights, lifted):
    planes, length = modes.shape[:2]
    mode_count = planes // 2
    frames = stashed.shape[0]
    pixels = float(length * length)
    height = 8
    steps = length // height
    pairs = [(i, j) for j in range(mode_count) for i in range(j + 1)]
    strict = [(i, j) for i, j in pairs if i < j]

    def fold(value):
        total = value[:, :128]
        for at in range(128, length, 128):
            total = total + value[:, at:at + 128]
        return total

    def at_rows(step):
        return pl.ds(pl.multiple_of(step * height, height), height)

    def gram_step(step, sums):
        rows = at_rows(step)
        raised = []
        for p in range(planes):
            value = modes[p, rows, :] + summed[p, rows, :] / root_total
            lifted[p, rows, :] = value
            raised.append(value)
        real, imag = raised[0::2], raised[1::2]
        terms = [fold(real[i] * real[j] + imag[i] * imag[j]) for i, j in pairs]
        terms += [fold(real[i] * imag[j] - imag[i] * real[j]) for i, j in strict]
        return tuple(a + b for a, b in zip(sums, terms))

    blank = jnp.zeros((height, 128), jnp.float32)
    sums = lax.fori_loop(0, steps, gram_step, (blank,) * (len(pairs) + len(strict)))

    def whole(value):
        return jnp.sum(jnp.sum(value, 0, keepdims=True), 1, keepdims=True)

    gram_real = {p: whole(s) / pixels for p, s in zip(pairs, sums)}
    gram_imag = {p: whole(s) / pixels for p, s in zip(strict, sums[len(pairs):])}
    upper_real, upper_imag = {}, {}
    for j in range(mode_count):
        for i in range(j):
            sum_real, sum_imag = gram_real[i, j], gram_imag[i, j]
            for k in range(i):
                a, b, c, d = upper_real[k, i], upper_imag[k, i], upper_real[k, j], upper_imag[k, j]
                sum_real = sum_real - (a * c + b * d)
                sum_imag = sum_imag - (a * d - b * c)
            upper_real[i, j] = sum_real / upper_real[i, i]
            upper_imag[i, j] = sum_imag / upper_real[i, i]
        diagonal = gram_real[j, j]
        for k in range(j):
            diagonal = diagonal - (upper_real[k, j] * upper_real[k, j] + upper_imag[k, j] * upper_imag[k, j])
        upper_real[j, j] = jnp.sqrt(diagonal)
    wide = {p: jnp.broadcast_to(v, (height, length)) for p, v in upper_real.items()}
    wide_imag = {p: jnp.broadcast_to(v, (height, length)) for p, v in upper_imag.items()}
    inverse = {j: jnp.broadcast_to(1.0 / upper_real[j, j], (height, length)) for j in range(mode_count)}

    def basis_step(step, carry):
        rows = at_rows(step)
        basis = []
        for j in range(mode_count):
            real, imag = lifted[2 * j, rows, :], lifted[2 * j + 1, rows, :]
            for i in range(j):
                a, b = wide[i, j], wide_imag[i, j]
                c, d = basis[i]
                real = real - (a * c - b * d)
                imag = imag - (a * d + b * c)
            real, imag = real * inverse[j], imag * inverse[j]
            basis.append((real, imag))
            new_modes[2 * j, rows, :] = real
            new_modes[2 * j + 1, rows, :] = imag
        return carry

    lax.fori_loop(0, steps, basis_step, 0)

    def fit_step(step, sums):
        rows = at_rows(step)
        basis = [new_modes[p, rows, :] for p in range(planes)]
        terms = []
        for j in range(mode_count):
            real, imag = modes[2 * j, rows, :], modes[2 * j + 1, rows, :]
            terms += [fold(basis[2 * k] * real + basis[2 * k + 1] * imag) for k in range(mode_count)]
        for g in range(frames):
            real, imag = stashed[g, 0, rows, :], stashed[g, 1, rows, :]
            terms += [fold(basis[2 * k] * real + basis[2 * k + 1] * imag) for k in range(mode_count)]
        return tuple(a + b for a, b in zip(sums, terms))

    sums = lax.fori_loop(0, steps, fit_step, (blank,) * (mode_count * (mode_count + frames)))
    sums = [whole(s) / pixels for s in sums]
    for g in range(frames):
        for k in range(mode_count):
            refit = 0.5 * sums[mode_count * (mode_count + g) + k]
            for j in range(mode_count):
                refit = refit + weights[g, j] * sums[mode_count * j + k]
            kept = jnp.full((1, 1), weights[g, k], jnp.float32)
            new_weights[g:g + 1, k:k + 1] = jnp.where(g < count[0], refit, kept)


def reach(device, source, target, send_sem, recv_sem):
    return pltpu.make_async_remote_copy(
        src_ref=source,
        dst_ref=target,
        send_sem=send_sem,
        recv_sem=recv_sem,
        device_id=device,
        device_id_type=pl.DeviceIdType.MESH,
    )


class Sides:
    def __init__(self, scan_count, col_count):
        self.scan, self.col = lax.axis_index("scan"), lax.axis_index("col")
        self.right = (self.scan, lax.rem(self.col + 1, col_count))
        self.left = (self.scan, lax.rem(self.col + col_count - 1, col_count))
        self.down = (lax.rem(self.scan + 1, scan_count), self.col)
        self.up = (lax.rem(self.scan + scan_count - 1, scan_count), self.col)
        self.has_right, self.has_left = self.col < col_count - 1, self.col > 0
        self.has_down, self.has_up = self.scan < scan_count - 1, self.scan > 0

    def all(self):
        return (
            (self.right, self.has_right), (self.left, self.has_left),
            (self.down, self.has_down), (self.up, self.has_up),
        )


def greet(sides, partners):
    barrier = pltpu.get_barrier_semaphore()
    for device in partners:
        pl.semaphore_signal(barrier, inc=1, device_id=device, device_id_type=pl.DeviceIdType.MESH)
    for device, there in sides.all():

        @pl.when(there)
        def _():
            pl.semaphore_signal(
                barrier, inc=1, device_id=device, device_id_type=pl.DeviceIdType.MESH
            )

    present = [there.astype(jnp.int32) for _, there in sides.all()]
    pl.semaphore_wait(barrier, len(partners) + sum(present))


class Shift:
    def __init__(self, copy, sends, receives):
        self.copy, self.sends, self.receives = copy, sends, receives

    def start(self):
        pl.when(self.sends)(self.copy.start)

    def arrive(self):
        pl.when(self.receives)(self.copy.wait_recv)

    def leave(self):
        pl.when(self.sends)(self.copy.wait_send)


def halo_shifts(sides, wide, height, width, send_sems, recv_sems):
    leftward = Shift(
        reach(
            sides.left, wide.at[:, pl.ds(0, height), pl.ds(0, width)],
            wide.at[:, pl.ds(0, height), pl.ds(width, width)], send_sems.at[0], recv_sems.at[0],
        ),
        sides.has_left, sides.has_right,
    )
    upward = Shift(
        reach(
            sides.up, wide.at[:, pl.ds(0, height), :], wide.at[:, pl.ds(height, height), :],
            send_sems.at[1], recv_sems.at[1],
        ),
        sides.has_up, sides.has_down,
    )
    return leftward, upward


def blank_edges(sides, wide, height, width):
    @pl.when(jnp.logical_not(sides.has_right))
    def _():
        wide[:, :height, width:] = jnp.zeros((wide.shape[0], height, width), jnp.float32)

    @pl.when(jnp.logical_not(sides.has_down))
    def _():
        wide[:, height:, :] = jnp.zeros((wide.shape[0], height, 2 * width), jnp.float32)


def halo_kernel(scan_count, col_count, field, wide, send_sems, recv_sems):
    height, width = field.shape[1:]
    sides = Sides(scan_count, col_count)
    blank_edges(sides, wide, height, width)
    wide[:, :height, :width] = field[...]
    greet(sides, [])
    leftward, upward = halo_shifts(sides, wide, height, width, send_sems, recv_sems)
    leftward.start()
    leftward.arrive()
    upward.start()
    upward.arrive()
    leftward.leave()
    upward.leave()


def orders(scan_count, col_count):
    scan_bits = [("scan", 1 << b) for b in range(scan_count.bit_length() - 1)]
    col_bits = [("col", 1 << b) for b in range(col_count.bit_length() - 1)]
    first, second = col_bits[:1], scan_bits[:1]
    third, rest = col_bits[1:], scan_bits[1:]
    return [first + second + third + rest, first + third + second + rest]


def exchange_kernel(
    scan_count, col_count, again, field, totals, terms, summed, result,
    partial, landed, sideways, fallen, bottom, send_sems, recv_sems, side_send, side_recv,
):
    height, width = field.shape[1:]
    sides = Sides(scan_count, col_count)
    streams = orders(scan_count, col_count)
    steps = len(streams[0])
    share = terms.shape[0] // len(streams)

    def partner(axis, bit):
        at = sides.scan if axis == "scan" else sides.col
        mine = at // bit % 2
        other = at + bit - 2 * bit * mine
        return mine, ((other, sides.col) if axis == "scan" else (sides.scan, other))

    def blank(ref, absent):
        @pl.when(absent)
        def _():
            ref[...] = jnp.zeros_like(ref)

    blank(sideways, jnp.logical_not(sides.has_left))
    blank(fallen, jnp.logical_not(sides.has_up))
    if again:
        blank_edges(sides, result, height, width)
    greet(sides, [partner(axis, bit)[1] for axis, bit in streams[0]])

    rightward = [
        Shift(
            reach(
                sides.right, totals.at[:, pl.ds(at, height), pl.ds(width, width)],
                sideways.at[:, pl.ds(at, height), :], side_send.at[k], side_recv.at[k],
            ),
            sides.has_right, sides.has_left,
        )
        for k, at in enumerate((height, 0))
    ]
    downward = Shift(
        reach(sides.down, bottom, fallen, side_send.at[2], side_recv.at[2]), sides.has_down, sides.has_up
    )
    if again:
        leftward, upward = halo_shifts(
            sides, result, height, width, side_send.at[pl.ds(3, 2)], side_recv.at[pl.ds(3, 2)]
        )

    bases = [[t * share] for t in range(len(streams))]
    halves = [share >> (s + 1) for s in range(steps)]
    copies = {}

    def rows(base, count):
        return pl.ds(pl.multiple_of(base, 8), count)

    def scatter_start(t, s):
        mine, device = partner(*streams[t][s])
        half = halves[s]
        base = bases[t][s]
        bases[t].append(base + mine * half)
        source = terms if s == 0 else partial
        copy = reach(
            device, source.at[rows(base + (1 - mine) * half, half), :],
            landed.at[pl.ds(t * share + share - 2 * half, half), :],
            send_sems.at[t, s], recv_sems.at[t, s],
        )
        copy.start()
        copies[t, s] = copy

    def scatter_finish(t, s):
        half = halves[s]
        copies[t, s].wait_recv()
        at = rows(bases[t][s + 1], half)
        source = terms if s == 0 else partial
        target = summed if s == steps - 1 else partial
        target[at, :] = source[at, :] + landed[pl.ds(t * share + share - 2 * half, half), :]

    def gather_start(t, s):
        _, device = partner(*streams[t][s])
        piece = summed.at[rows(bases[t][s + 1], halves[s]), :]
        copy = reach(device, piece, piece, send_sems.at[t, steps + s], recv_sems.at[t, steps + s])
        copy.start()
        copies[t, steps + s] = copy

    def drop():
        rightward[0].arrive()
        bottom[...] = totals[:, height:, :width] + sideways[:, height:, :]
        downward.start()

    def renew():
        rightward[1].arrive()
        downward.arrive()
        sums = totals[:, :height, :width] + sideways[:, :height, :] + fallen[...]
        fresh = field[...] + sums[:2] / (sums[2] + 1.0)
        result[:, :height, :width] = fresh
        if again:
            leftward.start()

    def lift():
        if again:
            leftward.arrive()
            upward.start()

    hooks = {1: drop, steps + steps // 2 - 1: renew, 2 * steps - 2: lift}
    every = range(len(streams))
    rightward[0].start()
    for t in every:
        scatter_start(t, 0)
    rightward[1].start()
    for s in range(steps):
        for t in every:
            scatter_finish(t, s)
            if s < steps - 1:
                scatter_start(t, s + 1)
            else:
                gather_start(t, s)
        if s in hooks:
            hooks[s]()
    for s in range(steps - 1, -1, -1):
        for t in every:
            copies[t, steps + s].wait_recv()
            if s > 0:
                gather_start(t, s - 1)
        if 2 * steps - 1 - s in hooks:
            hooks[2 * steps - 1 - s]()
    if again:
        upward.arrive()
    for copy in copies.values():
        copy.wait_send()
    for shift in rightward + [downward] + ([leftward, upward] if again else []):
        shift.leave()


def shape(*dims):
    return jax.ShapeDtypeStruct(dims, jnp.float32)


def on_device(object_field, amplitudes, positions, frame_count, coefficients, probe_modes):
    frames, length = amplitudes.shape[:2]
    mode_count = probe_modes.shape[0]
    planes = 2 * mode_count
    block_height, block_width = object_field.shape[1:]
    scan_count = lax.axis_size("scan")
    col_count = lax.axis_size("col")
    block_corner = jnp.stack(
        [lax.axis_index("scan") * block_height, lax.axis_index("col") * block_width]
    )
    offsets = positions - block_corner[None, :]
    root_total = math.sqrt(frames * scan_count * col_count)
    rows_table, cols_table = make_tables(length)
    modes = probe_modes.reshape(planes, length, length)
    full_height, full_width = block_height + length, block_width + length
    wide = pl.pallas_call(
        functools.partial(halo_kernel, scan_count, col_count),
        name="halo",
        out_shape=shape(2, full_height, full_width),
        in_specs=[VMEM],
        out_specs=VMEM,
        scratch_shapes=[pltpu.SemaphoreType.DMA((2,))] * 2,
        compiler_params=pltpu.CompilerParams(collective_id=ITERS, has_side_effects=True),
    )(object_field)
    for iteration in range(ITERS):
        again = iteration < ITERS - 1
        totals, mode_terms, stashed = pl.pallas_call(
            frames_kernel,
            name="frames",
            out_shape=(
                shape(3, full_height, full_width),
                shape(planes, length, length),
                shape(frames, 2, length, length),
            ),
            in_specs=[SMEM] * 3 + [VMEM] * 5,
            out_specs=(VMEM,) * 3,
            cost_estimate=pl.CostEstimate(flops=2 * 10**9, bytes_accessed=10**7, transcendentals=0),
        )(
            frame_count, offsets, coefficients, wide, amplitudes, modes, rows_table, cols_table,
        )
        steps = scan_count.bit_length() + col_count.bit_length() - 2
        rows = planes * length
        summed, result = pl.pallas_call(
            functools.partial(exchange_kernel, scan_count, col_count, again),
            name="exchange",
            out_shape=(
                shape(rows, length),
                shape(2, full_height, full_width) if again else shape(2, block_height, block_width),
            ),
            in_specs=[VMEM] * 3,
            out_specs=(VMEM,) * 2,
            scratch_shapes=[
                pltpu.VMEM((rows, length), jnp.float32),
                pltpu.VMEM((rows, length), jnp.float32),
                pltpu.VMEM((3, full_height, length), jnp.float32),
                pltpu.VMEM((3, length, block_width), jnp.float32),
                pltpu.VMEM((3, length, block_width), jnp.float32),
                pltpu.SemaphoreType.DMA((2, 2 * steps)),
                pltpu.SemaphoreType.DMA((2, 2 * steps)),
                pltpu.SemaphoreType.DMA((5,)),
                pltpu.SemaphoreType.DMA((5,)),
            ],
            compiler_params=pltpu.CompilerParams(collective_id=iteration, has_side_effects=True),
        )(object_field, totals, mode_terms.reshape(rows, length))
        if again:
            wide = result
            object_field = result[:, :block_height, :block_width]
        else:
            object_field = result
        summed = summed.reshape(planes, length, length)
        modes, coefficients = pl.pallas_call(
            lambda *refs: refit_kernel(root_total, *refs),
            name="refit",
            out_shape=(shape(planes, length, length), shape(frames, mode_count)),
            in_specs=[SMEM] * 2 + [VMEM] * 3,
            out_specs=(VMEM,) * 2,
            scratch_shapes=[pltpu.VMEM((planes, length, length), jnp.float32)],
        )(frame_count, coefficients, summed, modes, stashed)
    return (object_field, modes.reshape(probe_modes.shape), coefficients)


def solution(mesh):
    placed = (
        P(None, "scan", "col"),
        P(("scan", "col"), None, None),
        P(("scan", "col"), None),
        P(("scan", "col")),
        P(("scan", "col"), None),
        P(),
    )
    return jax.shard_map(
        on_device,
        mesh=mesh,
        in_specs=placed,
        out_specs=(P(None, "scan", "col"), P(), P(("scan", "col"), None)),
        check_vma=False,
    )
```

```python
import functools
import math

import jax
import jax.numpy as jnp
from jax import lax
from jax.experimental import pallas as pl
from jax.experimental.pallas import tpu as pltpu
from jax.sharding import PartitionSpec as P

ITERS = 2

VMEM = pl.BlockSpec(memory_space=pltpu.VMEM)
SMEM = pl.BlockSpec(memory_space=pltpu.SMEM)


def make_tables(length):
    indices = jnp.arange(length, dtype=jnp.int32)
    phases = indices[:, None] * indices[None, :] % length
    angles = phases.astype(jnp.float32) * (2.0 * math.pi / length)
    factor = 1.0 / math.sqrt(length)
    cosine = jnp.cos(angles) * factor
    sine_table = jnp.sin(angles) * factor
    rows_table = jnp.concatenate(
        [jnp.concatenate([cosine, sine_table], 1), jnp.concatenate([-sine_table, cosine], 1)], 0
    )
    cols_table = jnp.concatenate(
        [jnp.concatenate([cosine, -sine_table], 1), jnp.concatenate([sine_table, cosine], 1)], 0
    )
    return (rows_table.astype(jnp.bfloat16), cols_table.astype(jnp.bfloat16))


def apply_transform(stacked, first_table, second_table):
    length = stacked.shape[1]
    halfway = jnp.dot(first_table, stacked, preferred_element_type=jnp.float32).astype(jnp.bfloat16)
    beside = jnp.concatenate([halfway[:length], halfway[length:]], 1)
    return jnp.dot(beside, second_table, preferred_element_type=jnp.float32)


def frames_kernel(
    count, offsets, weights, wide, amplitudes, modes, rows_table, cols_table,
    totals, mode_terms, stashed,
):
    length = amplitudes.shape[1]
    mode_count = modes.shape[0] // 2
    full_width = wide.shape[2]
    block_width = full_width - length
    totals[...] = jnp.zeros_like(totals)
    mode_terms[...] = jnp.zeros_like(mode_terms)
    stashed[...] = jnp.zeros_like(stashed)

    def visit(slot, carry):
        row, col = offsets[slot, 0], offsets[slot, 1]
        start = pl.multiple_of(row // 8 * 8, 8)
        rest = row - start
        rows = pl.ds(start, length + 8)

        def cut(plane):
            band = wide[plane, rows, :]
            band = pltpu.roll(band, lax.rem(full_width - col, full_width), 1)[:, :length]
            return pltpu.roll(band, lax.rem(length + 8 - rest, length + 8), 0)[:length]

        def place(plane, piece):
            band = jnp.concatenate([piece, jnp.zeros((8, length), jnp.float32)], 0)
            band = pltpu.roll(band, rest, 0)
            band = jnp.concatenate([band, jnp.zeros((length + 8, block_width), jnp.float32)], 1)
            totals[plane, rows, :] += pltpu.roll(band, col, 1)

        object_real = cut(0)
        object_imag = cut(1)
        probe_real = weights[slot, 0] * modes[0]
        probe_imag = weights[slot, 0] * modes[1]
        for k in range(1, mode_count):
            probe_real += weights[slot, k] * modes[2 * k]
            probe_imag += weights[slot, k] * modes[2 * k + 1]
        place(2, probe_real * probe_real + probe_imag * probe_imag)
        exit_real = probe_real * object_real - probe_imag * object_imag
        exit_imag = probe_real * object_imag + probe_imag * object_real
        stacked = jnp.concatenate([exit_real, exit_imag], 0).astype(jnp.bfloat16)
        far = apply_transform(stacked, rows_table[...], cols_table[...])
        far_real, far_imag = far[:, :length], far[:, length:]
        magnitude = jnp.sqrt(far_real * far_real + far_imag * far_imag)
        factor = amplitudes[slot].astype(jnp.float32) / jnp.maximum(magnitude, 0.5)
        scaled = jnp.concatenate([far_real * factor, far_imag * factor], 0).astype(jnp.bfloat16)
        back = apply_transform(scaled, cols_table[...], rows_table[...])
        diff_real = back[:, :length] - exit_real
        diff_imag = back[:, length:] - exit_imag
        place(0, probe_real * diff_real + probe_imag * diff_imag)
        place(1, probe_real * diff_imag - probe_imag * diff_real)
        step_real = object_real * diff_real + object_imag * diff_imag
        step_imag = object_real * diff_imag - object_imag * diff_real
        stashed[slot, 0] = step_real
        stashed[slot, 1] = step_imag
        for k in range(mode_count):
            mode_terms[2 * k] += weights[slot, k] * step_real
            mode_terms[2 * k + 1] += weights[slot, k] * step_imag
        return carry

    lax.fori_loop(0, count[0], visit, 0)


def refit_kernel(root_total, count, weights, summed, modes, stashed, new_modes, new_weights, lifted):
    planes, length = modes.shape[:2]
    mode_count = planes // 2
    frames = stashed.shape[0]
    pixels = float(length * length)
    height = 8
    steps = length // height
    pairs = [(i, j) for j in range(mode_count) for i in range(j + 1)]
    strict = [(i, j) for i, j in pairs if i < j]

    def fold(value):
        total = value[:, :128]
        for at in range(128, length, 128):
            total = total + value[:, at:at + 128]
        return total

    def at_rows(step):
        return pl.ds(pl.multiple_of(step * height, height), height)

    def gram_step(step, sums):
        rows = at_rows(step)
        raised = []
        for p in range(planes):
            value = modes[p, rows, :] + summed[p, rows, :] / root_total
            lifted[p, rows, :] = value
            raised.append(value)
        real, imag = raised[0::2], raised[1::2]
        terms = [fold(real[i] * real[j] + imag[i] * imag[j]) for i, j in pairs]
        terms += [fold(real[i] * imag[j] - imag[i] * real[j]) for i, j in strict]
        return tuple(a + b for a, b in zip(sums, terms))

    blank = jnp.zeros((height, 128), jnp.float32)
    sums = lax.fori_loop(0, steps, gram_step, (blank,) * (len(pairs) + len(strict)))

    def whole(value):
        return jnp.sum(jnp.sum(value, 0, keepdims=True), 1, keepdims=True)

    gram_real = {p: whole(s) / pixels for p, s in zip(pairs, sums)}
    gram_imag = {p: whole(s) / pixels for p, s in zip(strict, sums[len(pairs):])}
    upper_real, upper_imag = {}, {}
    for j in range(mode_count):
        for i in range(j):
            sum_real, sum_imag = gram_real[i, j], gram_imag[i, j]
            for k in range(i):
                a, b, c, d = upper_real[k, i], upper_imag[k, i], upper_real[k, j], upper_imag[k, j]
                sum_real = sum_real - (a * c + b * d)
                sum_imag = sum_imag - (a * d - b * c)
            upper_real[i, j] = sum_real / upper_real[i, i]
            upper_imag[i, j] = sum_imag / upper_real[i, i]
        diagonal = gram_real[j, j]
        for k in range(j):
            diagonal = diagonal - (upper_real[k, j] * upper_real[k, j] + upper_imag[k, j] * upper_imag[k, j])
        upper_real[j, j] = jnp.sqrt(diagonal)
    wide = {p: jnp.broadcast_to(v, (height, length)) for p, v in upper_real.items()}
    wide_imag = {p: jnp.broadcast_to(v, (height, length)) for p, v in upper_imag.items()}
    inverse = {j: jnp.broadcast_to(1.0 / upper_real[j, j], (height, length)) for j in range(mode_count)}

    def basis_step(step, carry):
        rows = at_rows(step)
        basis = []
        for j in range(mode_count):
            real, imag = lifted[2 * j, rows, :], lifted[2 * j + 1, rows, :]
            for i in range(j):
                a, b = wide[i, j], wide_imag[i, j]
                c, d = basis[i]
                real = real - (a * c - b * d)
                imag = imag - (a * d + b * c)
            real, imag = real * inverse[j], imag * inverse[j]
            basis.append((real, imag))
            new_modes[2 * j, rows, :] = real
            new_modes[2 * j + 1, rows, :] = imag
        return carry

    lax.fori_loop(0, steps, basis_step, 0)

    def fit_step(step, sums):
        rows = at_rows(step)
        basis = [new_modes[p, rows, :] for p in range(planes)]
        terms = []
        for j in range(mode_count):
            real, imag = modes[2 * j, rows, :], modes[2 * j + 1, rows, :]
            terms += [fold(basis[2 * k] * real + basis[2 * k + 1] * imag) for k in range(mode_count)]
        for g in range(frames):
            real, imag = stashed[g, 0, rows, :], stashed[g, 1, rows, :]
            terms += [fold(basis[2 * k] * real + basis[2 * k + 1] * imag) for k in range(mode_count)]
        return tuple(a + b for a, b in zip(sums, terms))

    sums = lax.fori_loop(0, steps, fit_step, (blank,) * (mode_count * (mode_count + frames)))
    sums = [whole(s) / pixels for s in sums]
    for g in range(frames):
        for k in range(mode_count):
            refit = 0.5 * sums[mode_count * (mode_count + g) + k]
            for j in range(mode_count):
                refit = refit + weights[g, j] * sums[mode_count * j + k]
            kept = jnp.full((1, 1), weights[g, k], jnp.float32)
            new_weights[g:g + 1, k:k + 1] = jnp.where(g < count[0], refit, kept)


def reach(device, source, target, send_sem, recv_sem):
    return pltpu.make_async_remote_copy(
        src_ref=source,
        dst_ref=target,
        send_sem=send_sem,
        recv_sem=recv_sem,
        device_id=device,
        device_id_type=pl.DeviceIdType.MESH,
    )


class Sides:
    def __init__(self, scan_count, col_count):
        self.scan, self.col = lax.axis_index("scan"), lax.axis_index("col")
        self.right = (self.scan, lax.rem(self.col + 1, col_count))
        self.left = (self.scan, lax.rem(self.col + col_count - 1, col_count))
        self.down = (lax.rem(self.scan + 1, scan_count), self.col)
        self.up = (lax.rem(self.scan + scan_count - 1, scan_count), self.col)
        self.has_right, self.has_left = self.col < col_count - 1, self.col > 0
        self.has_down, self.has_up = self.scan < scan_count - 1, self.scan > 0

    def all(self):
        return (
            (self.right, self.has_right), (self.left, self.has_left),
            (self.down, self.has_down), (self.up, self.has_up),
        )


def greet(sides, partners):
    barrier = pltpu.get_barrier_semaphore()
    for device in partners:
        pl.semaphore_signal(barrier, inc=1, device_id=device, device_id_type=pl.DeviceIdType.MESH)
    for device, there in sides.all():

        @pl.when(there)
        def _():
            pl.semaphore_signal(
                barrier, inc=1, device_id=device, device_id_type=pl.DeviceIdType.MESH
            )

    present = [there.astype(jnp.int32) for _, there in sides.all()]
    pl.semaphore_wait(barrier, len(partners) + sum(present))


class Shift:
    def __init__(self, copy, sends, receives):
        self.copy, self.sends, self.receives = copy, sends, receives

    def start(self):
        pl.when(self.sends)(self.copy.start)

    def arrive(self):
        pl.when(self.receives)(self.copy.wait_recv)

    def leave(self):
        pl.when(self.sends)(self.copy.wait_send)


class Halo:
    def __init__(self, sides, wide, height, width, send_sems, recv_sems):
        top, low = pl.ds(0, height), pl.ds(height, height)
        near, far = pl.ds(0, width), pl.ds(width, width)
        planes = range(wide.shape[0])

        def shift(device, source, target, at, sends, receives):
            copy = reach(device, source, target, send_sems.at[at], recv_sems.at[at])
            return Shift(copy, sends, receives)

        self.side = shift(
            sides.left, wide.at[:, top, near], wide.at[:, top, far], 0, sides.has_left, sides.has_right
        )
        self.up = [
            shift(
                sides.up, wide.at[p, top, near], wide.at[p, low, near], 1 + 2 * p,
                sides.has_up, sides.has_down,
            )
            for p in planes
        ]
        self.corner = [
            shift(
                sides.left, wide.at[p, low, near], wide.at[p, low, far], 2 + 2 * p,
                sides.has_left, sides.has_right,
            )
            for p in planes
        ]

    def begin(self):
        for up in self.up:
            up.start()
        self.side.start()

    def turn(self, plane):
        self.up[plane].arrive()
        self.corner[plane].start()

    def end(self):
        self.side.arrive()
        for corner in self.corner:
            corner.arrive()
        for shift in [self.side] + self.up + self.corner:
            shift.leave()


def blank_edges(sides, wide, height, width):
    @pl.when(jnp.logical_not(sides.has_right))
    def _():
        wide[:, :, width:] = jnp.zeros((wide.shape[0], 2 * height, width), jnp.float32)

    @pl.when(jnp.logical_not(sides.has_down))
    def _():
        wide[:, height:, :width] = jnp.zeros((wide.shape[0], height, width), jnp.float32)


def halo_kernel(scan_count, col_count, field, wide, send_sems, recv_sems):
    height, width = field.shape[1:]
    sides = Sides(scan_count, col_count)
    blank_edges(sides, wide, height, width)
    wide[:, :height, :width] = field[...]
    greet(sides, [])
    halo = Halo(sides, wide, height, width, send_sems, recv_sems)
    halo.begin()
    for plane in range(wide.shape[0]):
        halo.turn(plane)
    halo.end()


def orders(scan_count, col_count):
    scan_bits = [("scan", 1 << b) for b in range(scan_count.bit_length() - 1)]
    col_bits = [("col", 1 << b) for b in range(col_count.bit_length() - 1)]
    core, col = col_bits[:1], col_bits[1:]
    near, middle, far = scan_bits[:1], scan_bits[1:2], scan_bits[2:]
    return [
        core + col + near + middle + far,
        core + middle + col + near + far,
        core + near + col + middle + far,
        core + col + middle + near + far,
    ]


def exchange_kernel(
    scan_count, col_count, again, field, totals, terms, summed, result,
    partial, landed, sideways, fallen, bottom, send_sems, recv_sems, side_send, side_recv,
):
    height, width = bottom.shape[1:]
    sides = Sides(scan_count, col_count)
    streams = orders(scan_count, col_count)
    steps = len(streams[0])
    if terms.shape[0] // len(streams) >> steps < 8:
        streams = streams[1:3]
    share = terms.shape[0] // len(streams)

    def partner(axis, bit):
        at = sides.scan if axis == "scan" else sides.col
        mine = at // bit % 2
        other = at + bit - 2 * bit * mine
        return mine, ((other, sides.col) if axis == "scan" else (sides.scan, other))

    def blank(ref, absent):
        @pl.when(absent)
        def _():
            ref[...] = jnp.zeros_like(ref)

    blank(sideways, jnp.logical_not(sides.has_left))
    blank(fallen, jnp.logical_not(sides.has_up))
    if again:
        blank_edges(sides, result, height, width)
    greet(sides, [partner(axis, bit)[1] for axis, bit in streams[0]])

    def rightward(at, band, target):
        copy = reach(sides.right, band, target, side_send.at[at], side_recv.at[at])
        return Shift(copy, sides.has_right, sides.has_left)

    sums = range(totals.shape[0])
    top, low = pl.ds(0, height), pl.ds(height, height)
    beside = pl.ds(width, width)
    rights = [rightward(p, totals.at[p, low, beside], sideways.at[p, low, :]) for p in sums]
    last_right = rightward(3, totals.at[:, top, beside], sideways.at[:, top, :])
    downs = [
        Shift(
            reach(sides.down, bottom.at[p], fallen.at[p], side_send.at[4 + p], side_recv.at[4 + p]),
            sides.has_down, sides.has_up,
        )
        for p in sums
    ]
    if again:
        halo = Halo(sides, result, height, width, side_send.at[pl.ds(7, 5)], side_recv.at[pl.ds(7, 5)])

    bases = [[t * share] for t in range(len(streams))]
    halves = [share >> (s + 1) for s in range(steps)]
    copies = {}

    def rows(base, count):
        return pl.ds(pl.multiple_of(base, 8), count)

    def scatter_start(t, s):
        mine, device = partner(*streams[t][s])
        half = halves[s]
        base = bases[t][s]
        bases[t].append(base + mine * half)
        source = terms if s == 0 else partial
        copy = reach(
            device, source.at[rows(base + (1 - mine) * half, half), :],
            landed.at[pl.ds(t * share + share - 2 * half, half), :],
            send_sems.at[t, s], recv_sems.at[t, s],
        )
        copy.start()
        copies[t, s] = copy

    def scatter_finish(t, s):
        half = halves[s]
        copies[t, s].wait_recv()
        at = rows(bases[t][s + 1], half)
        source = terms if s == 0 else partial
        target = summed if s == steps - 1 else partial
        target[at, :] = source[at, :] + landed[pl.ds(t * share + share - 2 * half, half), :]

    def gather_start(t, s):
        _, device = partner(*streams[t][s])
        piece = summed.at[rows(bases[t][s + 1], halves[s]), :]
        copy = reach(device, piece, piece, send_sems.at[t, steps + s], recv_sems.at[t, steps + s])
        copy.start()
        copies[t, steps + s] = copy

    def drop(p):
        rights[p].arrive()
        bottom[p] = totals[p, height:, :width] + sideways[p, height:, :]
        downs[p].start()

    def renew():
        last_right.arrive()
        for down in downs:
            down.arrive()
        update = totals[:, :height, :width] + sideways[:, :height, :] + fallen[...]
        result[:, :height, :width] = field[:, :height, :width] + update[:2] / (update[2] + 1.0)
        if again:
            halo.begin()

    def turn(p):
        if again:
            halo.turn(p)

    hooks = {
        0: [lambda: drop(0)],
        1: [lambda: drop(1), lambda: drop(2)],
        steps: [renew],
        2 * steps - 3: [lambda: turn(0)],
        2 * steps - 2: [lambda: turn(1)],
    }

    def run_hooks(at):
        for hook in hooks.get(at, ()):
            hook()

    every = range(len(streams))
    for right in rights:
        right.start()
    for t in every:
        scatter_start(t, 0)
    last_right.start()
    for s in range(steps):
        for t in every:
            scatter_finish(t, s)
            if s < steps - 1:
                scatter_start(t, s + 1)
            else:
                gather_start(t, s)
        run_hooks(s)
    for s in range(steps - 1, -1, -1):
        for t in every:
            copies[t, steps + s].wait_recv()
            if s > 0:
                gather_start(t, s - 1)
        run_hooks(2 * steps - 1 - s)
    for copy in copies.values():
        copy.wait_send()
    for shift in rights + [last_right] + downs:
        shift.leave()
    if again:
        halo.end()


def shape(*dims):
    return jax.ShapeDtypeStruct(dims, jnp.float32)


def on_device(object_field, amplitudes, positions, frame_count, coefficients, probe_modes):
    frames, length = amplitudes.shape[:2]
    mode_count = probe_modes.shape[0]
    planes = 2 * mode_count
    block_height, block_width = object_field.shape[1:]
    scan_count = lax.axis_size("scan")
    col_count = lax.axis_size("col")
    block_corner = jnp.stack(
        [lax.axis_index("scan") * block_height, lax.axis_index("col") * block_width]
    )
    offsets = positions - block_corner[None, :]
    root_total = math.sqrt(frames * scan_count * col_count)
    rows_table, cols_table = make_tables(length)
    modes = probe_modes.reshape(planes, length, length)
    full_height, full_width = block_height + length, block_width + length
    wide = pl.pallas_call(
        functools.partial(halo_kernel, scan_count, col_count),
        name="halo",
        out_shape=shape(2, full_height, full_width),
        in_specs=[VMEM],
        out_specs=VMEM,
        scratch_shapes=[pltpu.SemaphoreType.DMA((5,))] * 2,
        compiler_params=pltpu.CompilerParams(collective_id=ITERS, has_side_effects=True),
    )(object_field)
    for iteration in range(ITERS):
        again = iteration < ITERS - 1
        totals, mode_terms, stashed = pl.pallas_call(
            frames_kernel,
            name="frames",
            out_shape=(
                shape(3, full_height, full_width),
                shape(planes, length, length),
                shape(frames, 2, length, length),
            ),
            in_specs=[SMEM] * 3 + [VMEM] * 5,
            out_specs=(VMEM,) * 3,
            cost_estimate=pl.CostEstimate(flops=2 * 10**9, bytes_accessed=10**7, transcendentals=0),
        )(
            frame_count, offsets, coefficients, wide, amplitudes, modes, rows_table, cols_table,
        )
        steps = scan_count.bit_length() + col_count.bit_length() - 2
        rows = planes * length
        summed, result = pl.pallas_call(
            functools.partial(exchange_kernel, scan_count, col_count, again),
            name="exchange",
            out_shape=(
                shape(rows, length),
                shape(2, full_height, full_width) if again else shape(2, block_height, block_width),
            ),
            in_specs=[VMEM] * 3,
            out_specs=(VMEM,) * 2,
            scratch_shapes=[
                pltpu.VMEM((rows, length), jnp.float32),
                pltpu.VMEM((rows, length), jnp.float32),
                pltpu.VMEM((3, full_height, length), jnp.float32),
                pltpu.VMEM((3, length, block_width), jnp.float32),
                pltpu.VMEM((3, length, block_width), jnp.float32),
                pltpu.SemaphoreType.DMA((4, 2 * steps)),
                pltpu.SemaphoreType.DMA((4, 2 * steps)),
                pltpu.SemaphoreType.DMA((12,)),
                pltpu.SemaphoreType.DMA((12,)),
            ],
            compiler_params=pltpu.CompilerParams(collective_id=iteration, has_side_effects=True),
        )(wide, totals, mode_terms.reshape(rows, length))
        wide = result
        summed = summed.reshape(planes, length, length)
        modes, coefficients = pl.pallas_call(
            lambda *refs: refit_kernel(root_total, *refs),
            name="refit",
            out_shape=(shape(planes, length, length), shape(frames, mode_count)),
            in_specs=[SMEM] * 2 + [VMEM] * 3,
            out_specs=(VMEM,) * 2,
            scratch_shapes=[pltpu.VMEM((planes, length, length), jnp.float32)],
        )(frame_count, coefficients, summed, modes, stashed)
    return (wide, modes.reshape(probe_modes.shape), coefficients)


def solution(mesh):
    placed = (
        P(None, "scan", "col"),
        P(("scan", "col"), None, None),
        P(("scan", "col"), None),
        P(("scan", "col")),
        P(("scan", "col"), None),
        P(),
    )
    return jax.shard_map(
        on_device,
        mesh=mesh,
        in_specs=placed,
        out_specs=(P(None, "scan", "col"), P(), P(("scan", "col"), None)),
        check_vma=False,
    )
```

```python
import functools
import math

import jax
import jax.numpy as jnp
from jax import lax
from jax.experimental import pallas as pl
from jax.experimental.pallas import tpu as pltpu
from jax.sharding import PartitionSpec as P

ITERS = 2

VMEM = pl.BlockSpec(memory_space=pltpu.VMEM)
SMEM = pl.BlockSpec(memory_space=pltpu.SMEM)


def make_tables(length):
    indices = jnp.arange(length, dtype=jnp.int32)
    phases = indices[:, None] * indices[None, :] % length
    angles = phases.astype(jnp.float32) * (2.0 * math.pi / length)
    factor = 1.0 / math.sqrt(length)
    cosine = jnp.cos(angles) * factor
    sine_table = jnp.sin(angles) * factor
    rows_table = jnp.concatenate(
        [jnp.concatenate([cosine, sine_table], 1), jnp.concatenate([-sine_table, cosine], 1)], 0
    )
    cols_table = jnp.concatenate(
        [jnp.concatenate([cosine, -sine_table], 1), jnp.concatenate([sine_table, cosine], 1)], 0
    )
    return (rows_table.astype(jnp.bfloat16), cols_table.astype(jnp.bfloat16))


def apply_transform(stacked, first_table, second_table):
    length = stacked.shape[1]
    halfway = jnp.dot(first_table, stacked, preferred_element_type=jnp.float32).astype(jnp.bfloat16)
    beside = jnp.concatenate([halfway[:length], halfway[length:]], 1)
    return jnp.dot(beside, second_table, preferred_element_type=jnp.float32)


def frames_kernel(
    count, offsets, weights, wide, amplitudes, modes, rows_table, cols_table,
    totals, mode_terms, stashed,
):
    length = amplitudes.shape[1]
    mode_count = modes.shape[0] // 2
    full_width = wide.shape[2]
    block_width = full_width - length
    totals[...] = jnp.zeros_like(totals)
    mode_terms[...] = jnp.zeros_like(mode_terms)
    stashed[...] = jnp.zeros_like(stashed)

    def visit(slot, carry):
        row, col = offsets[slot, 0], offsets[slot, 1]
        start = pl.multiple_of(row // 8 * 8, 8)
        rest = row - start
        rows = pl.ds(start, length + 8)

        def cut(plane):
            band = wide[plane, rows, :]
            band = pltpu.roll(band, lax.rem(full_width - col, full_width), 1)[:, :length]
            return pltpu.roll(band, lax.rem(length + 8 - rest, length + 8), 0)[:length]

        def place(plane, piece):
            band = jnp.concatenate([piece, jnp.zeros((8, length), jnp.float32)], 0)
            band = pltpu.roll(band, rest, 0)
            band = jnp.concatenate([band, jnp.zeros((length + 8, block_width), jnp.float32)], 1)
            totals[plane, rows, :] += pltpu.roll(band, col, 1)

        object_real = cut(0)
        object_imag = cut(1)
        probe_real = weights[slot, 0] * modes[0]
        probe_imag = weights[slot, 0] * modes[1]
        for k in range(1, mode_count):
            probe_real += weights[slot, k] * modes[2 * k]
            probe_imag += weights[slot, k] * modes[2 * k + 1]
        place(2, probe_real * probe_real + probe_imag * probe_imag)
        exit_real = probe_real * object_real - probe_imag * object_imag
        exit_imag = probe_real * object_imag + probe_imag * object_real
        stacked = jnp.concatenate([exit_real, exit_imag], 0).astype(jnp.bfloat16)
        far = apply_transform(stacked, rows_table[...], cols_table[...])
        far_real, far_imag = far[:, :length], far[:, length:]
        magnitude = jnp.sqrt(far_real * far_real + far_imag * far_imag)
        factor = amplitudes[slot].astype(jnp.float32) / jnp.maximum(magnitude, 0.5)
        scaled = jnp.concatenate([far_real * factor, far_imag * factor], 0).astype(jnp.bfloat16)
        back = apply_transform(scaled, cols_table[...], rows_table[...])
        diff_real = back[:, :length] - exit_real
        diff_imag = back[:, length:] - exit_imag
        place(0, probe_real * diff_real + probe_imag * diff_imag)
        place(1, probe_real * diff_imag - probe_imag * diff_real)
        step_real = object_real * diff_real + object_imag * diff_imag
        step_imag = object_real * diff_imag - object_imag * diff_real
        stashed[slot, 0] = step_real
        stashed[slot, 1] = step_imag
        for k in range(mode_count):
            mode_terms[2 * k] += weights[slot, k] * step_real
            mode_terms[2 * k + 1] += weights[slot, k] * step_imag
        return carry

    lax.fori_loop(0, count[0], visit, 0)


def refit_kernel(root_total, count, weights, summed, modes, stashed, new_modes, new_weights, lifted):
    planes, length = modes.shape[:2]
    mode_count = planes // 2
    frames = stashed.shape[0]
    pixels = float(length * length)
    height = 8
    steps = length // height
    pairs = [(i, j) for j in range(mode_count) for i in range(j + 1)]
    strict = [(i, j) for i, j in pairs if i < j]

    def fold(value):
        total = value[:, :128]
        for at in range(128, length, 128):
            total = total + value[:, at:at + 128]
        return total

    def at_rows(step):
        return pl.ds(pl.multiple_of(step * height, height), height)

    def gram_step(step, sums):
        rows = at_rows(step)
        raised = []
        for p in range(planes):
            value = modes[p, rows, :] + summed[p, rows, :] / root_total
            lifted[p, rows, :] = value
            raised.append(value)
        real, imag = raised[0::2], raised[1::2]
        terms = [fold(real[i] * real[j] + imag[i] * imag[j]) for i, j in pairs]
        terms += [fold(real[i] * imag[j] - imag[i] * real[j]) for i, j in strict]
        return tuple(a + b for a, b in zip(sums, terms))

    blank = jnp.zeros((height, 128), jnp.float32)
    sums = lax.fori_loop(0, steps, gram_step, (blank,) * (len(pairs) + len(strict)))

    def whole(value):
        return jnp.sum(jnp.sum(value, 0, keepdims=True), 1, keepdims=True)

    gram_real = {p: whole(s) / pixels for p, s in zip(pairs, sums)}
    gram_imag = {p: whole(s) / pixels for p, s in zip(strict, sums[len(pairs):])}
    upper_real, upper_imag = {}, {}
    for j in range(mode_count):
        for i in range(j):
            sum_real, sum_imag = gram_real[i, j], gram_imag[i, j]
            for k in range(i):
                a, b, c, d = upper_real[k, i], upper_imag[k, i], upper_real[k, j], upper_imag[k, j]
                sum_real = sum_real - (a * c + b * d)
                sum_imag = sum_imag - (a * d - b * c)
            upper_real[i, j] = sum_real / upper_real[i, i]
            upper_imag[i, j] = sum_imag / upper_real[i, i]
        diagonal = gram_real[j, j]
        for k in range(j):
            diagonal = diagonal - (upper_real[k, j] * upper_real[k, j] + upper_imag[k, j] * upper_imag[k, j])
        upper_real[j, j] = jnp.sqrt(diagonal)
    wide = {p: jnp.broadcast_to(v, (height, length)) for p, v in upper_real.items()}
    wide_imag = {p: jnp.broadcast_to(v, (height, length)) for p, v in upper_imag.items()}
    inverse = {j: jnp.broadcast_to(1.0 / upper_real[j, j], (height, length)) for j in range(mode_count)}

    def basis_step(step, carry):
        rows = at_rows(step)
        basis = []
        for j in range(mode_count):
            real, imag = lifted[2 * j, rows, :], lifted[2 * j + 1, rows, :]
            for i in range(j):
                a, b = wide[i, j], wide_imag[i, j]
                c, d = basis[i]
                real = real - (a * c - b * d)
                imag = imag - (a * d + b * c)
            real, imag = real * inverse[j], imag * inverse[j]
            basis.append((real, imag))
            new_modes[2 * j, rows, :] = real
            new_modes[2 * j + 1, rows, :] = imag
        return carry

    lax.fori_loop(0, steps, basis_step, 0)

    def fit_step(step, sums):
        rows = at_rows(step)
        basis = [new_modes[p, rows, :] for p in range(planes)]
        terms = []
        for j in range(mode_count):
            real, imag = modes[2 * j, rows, :], modes[2 * j + 1, rows, :]
            terms += [fold(basis[2 * k] * real + basis[2 * k + 1] * imag) for k in range(mode_count)]
        for g in range(frames):
            real, imag = stashed[g, 0, rows, :], stashed[g, 1, rows, :]
            terms += [fold(basis[2 * k] * real + basis[2 * k + 1] * imag) for k in range(mode_count)]
        return tuple(a + b for a, b in zip(sums, terms))

    sums = lax.fori_loop(0, steps, fit_step, (blank,) * (mode_count * (mode_count + frames)))
    sums = [whole(s) / pixels for s in sums]
    for g in range(frames):
        for k in range(mode_count):
            refit = 0.5 * sums[mode_count * (mode_count + g) + k]
            for j in range(mode_count):
                refit = refit + weights[g, j] * sums[mode_count * j + k]
            kept = jnp.full((1, 1), weights[g, k], jnp.float32)
            new_weights[g:g + 1, k:k + 1] = jnp.where(g < count[0], refit, kept)


def reach(device, source, target, send_sem, recv_sem):
    return pltpu.make_async_remote_copy(
        src_ref=source,
        dst_ref=target,
        send_sem=send_sem,
        recv_sem=recv_sem,
        device_id=device,
        device_id_type=pl.DeviceIdType.MESH,
    )


class Sides:
    def __init__(self, scan_count, col_count):
        self.scan, self.col = lax.axis_index("scan"), lax.axis_index("col")
        self.right = (self.scan, lax.rem(self.col + 1, col_count))
        self.left = (self.scan, lax.rem(self.col + col_count - 1, col_count))
        self.down = (lax.rem(self.scan + 1, scan_count), self.col)
        self.up = (lax.rem(self.scan + scan_count - 1, scan_count), self.col)
        self.has_right, self.has_left = self.col < col_count - 1, self.col > 0
        self.has_down, self.has_up = self.scan < scan_count - 1, self.scan > 0

    def all(self):
        return (
            (self.right, self.has_right), (self.left, self.has_left),
            (self.down, self.has_down), (self.up, self.has_up),
        )


def greet(sides, partners):
    barrier = pltpu.get_barrier_semaphore()
    for device in partners:
        pl.semaphore_signal(barrier, inc=1, device_id=device, device_id_type=pl.DeviceIdType.MESH)
    for device, there in sides.all():

        @pl.when(there)
        def _():
            pl.semaphore_signal(
                barrier, inc=1, device_id=device, device_id_type=pl.DeviceIdType.MESH
            )

    present = [there.astype(jnp.int32) for _, there in sides.all()]
    pl.semaphore_wait(barrier, len(partners) + sum(present))


class Shift:
    def __init__(self, copy, sends, receives):
        self.copy, self.sends, self.receives = copy, sends, receives

    def start(self):
        pl.when(self.sends)(self.copy.start)

    def arrive(self):
        pl.when(self.receives)(self.copy.wait_recv)

    def leave(self):
        pl.when(self.sends)(self.copy.wait_send)


class Halo:
    def __init__(self, sides, wide, height, width, send_sems, recv_sems):
        top, low = pl.ds(0, height), pl.ds(height, height)
        near, far = pl.ds(0, width), pl.ds(width, width)
        planes = range(wide.shape[0])

        def shift(device, source, target, at, sends, receives):
            copy = reach(device, source, target, send_sems.at[at], recv_sems.at[at])
            return Shift(copy, sends, receives)

        self.side = shift(
            sides.left, wide.at[:, top, near], wide.at[:, top, far], 0, sides.has_left, sides.has_right
        )
        self.up = [
            shift(
                sides.up, wide.at[p, top, near], wide.at[p, low, near], 1 + 2 * p,
                sides.has_up, sides.has_down,
            )
            for p in planes
        ]
        self.corner = [
            shift(
                sides.left, wide.at[p, low, near], wide.at[p, low, far], 2 + 2 * p,
                sides.has_left, sides.has_right,
            )
            for p in planes
        ]

    def begin(self):
        for up in self.up:
            up.start()
        self.side.start()

    def turn(self, plane):
        self.up[plane].arrive()
        self.corner[plane].start()

    def end(self):
        self.side.arrive()
        for corner in self.corner:
            corner.arrive()
        for shift in [self.side] + self.up + self.corner:
            shift.leave()


def blank_edges(sides, wide, height, width):
    @pl.when(jnp.logical_not(sides.has_right))
    def _():
        wide[:, :, width:] = jnp.zeros((wide.shape[0], 2 * height, width), jnp.float32)

    @pl.when(jnp.logical_not(sides.has_down))
    def _():
        wide[:, height:, :width] = jnp.zeros((wide.shape[0], height, width), jnp.float32)


def halo_kernel(scan_count, col_count, field, wide, send_sems, recv_sems):
    height, width = field.shape[1:]
    sides = Sides(scan_count, col_count)
    blank_edges(sides, wide, height, width)
    wide[:, :height, :width] = field[...]
    greet(sides, [])
    halo = Halo(sides, wide, height, width, send_sems, recv_sems)
    halo.begin()
    for plane in range(wide.shape[0]):
        halo.turn(plane)
    halo.end()


def orders(scan_count, col_count):
    scan_bits = [("scan", 1 << b) for b in range(scan_count.bit_length() - 1)]
    col_bits = [("col", 1 << b) for b in range(col_count.bit_length() - 1)]
    core, col = col_bits[:1], col_bits[1:]
    near, middle, far = scan_bits[:1], scan_bits[1:2], scan_bits[2:]
    return [
        core + col + near + middle + far,
        core + middle + col + near + far,
        core + near + col + middle + far,
        core + col + middle + near + far,
    ]


def exchange_kernel(
    scan_count, col_count, again, field, totals, terms, summed, result,
    partial, landed, sideways, fallen, bottom, send_sems, recv_sems, side_send, side_recv,
):
    height, width = bottom.shape[1:]
    sides = Sides(scan_count, col_count)
    streams = orders(scan_count, col_count)
    steps = len(streams[0])
    if terms.shape[0] // len(streams) >> steps < 8:
        streams = streams[1:3]
    share = terms.shape[0] // len(streams)

    def partner(axis, bit):
        at = sides.scan if axis == "scan" else sides.col
        mine = at // bit % 2
        other = at + bit - 2 * bit * mine
        return mine, ((other, sides.col) if axis == "scan" else (sides.scan, other))

    def blank(ref, absent):
        @pl.when(absent)
        def _():
            ref[...] = jnp.zeros_like(ref)

    blank(sideways, jnp.logical_not(sides.has_left))
    blank(fallen, jnp.logical_not(sides.has_up))
    if again:
        blank_edges(sides, result, height, width)
    greet(sides, [partner(axis, bit)[1] for axis, bit in streams[0]])

    def rightward(at, band, target):
        copy = reach(sides.right, band, target, side_send.at[at], side_recv.at[at])
        return Shift(copy, sides.has_right, sides.has_left)

    sums = range(totals.shape[0])
    top, low = pl.ds(0, height), pl.ds(height, height)
    beside = pl.ds(width, width)
    rights = [rightward(p, totals.at[p, low, beside], sideways.at[p, low, :]) for p in sums]
    last_right = rightward(3, totals.at[:, top, beside], sideways.at[:, top, :])
    downs = [
        Shift(
            reach(sides.down, bottom.at[p], fallen.at[p], side_send.at[4 + p], side_recv.at[4 + p]),
            sides.has_down, sides.has_up,
        )
        for p in sums
    ]
    if again:
        halo = Halo(sides, result, height, width, side_send.at[pl.ds(7, 5)], side_recv.at[pl.ds(7, 5)])

    bases = [[t * share] for t in range(len(streams))]
    halves = [share >> (s + 1) for s in range(steps)]
    copies = {}

    def rows(base, count):
        return pl.ds(pl.multiple_of(base, 8), count)

    def scatter_start(t, s):
        mine, device = partner(*streams[t][s])
        half = halves[s]
        base = bases[t][s]
        bases[t].append(base + mine * half)
        source = terms if s == 0 else partial
        copy = reach(
            device, source.at[rows(base + (1 - mine) * half, half), :],
            landed.at[pl.ds(t * share + share - 2 * half, half), :],
            send_sems.at[t, s], recv_sems.at[t, s],
        )
        copy.start()
        copies[t, s] = copy

    def scatter_finish(t, s):
        half = halves[s]
        copies[t, s].wait_recv()
        at = rows(bases[t][s + 1], half)
        source = terms if s == 0 else partial
        target = summed if s == steps - 1 else partial
        target[at, :] = source[at, :] + landed[pl.ds(t * share + share - 2 * half, half), :]

    def gather_start(t, s):
        _, device = partner(*streams[t][s])
        piece = summed.at[rows(bases[t][s + 1], halves[s]), :]
        copy = reach(device, piece, piece, send_sems.at[t, steps + s], recv_sems.at[t, steps + s])
        copy.start()
        copies[t, steps + s] = copy

    def drop(p):
        rights[p].arrive()
        bottom[p] = totals[p, height:, :width] + sideways[p, height:, :]
        downs[p].start()

    def renew():
        last_right.arrive()
        for down in downs:
            down.arrive()
        update = totals[:, :height, :width] + sideways[:, :height, :] + fallen[...]
        result[:, :height, :width] = field[:, :height, :width] + update[:2] / (update[2] + 1.0)
        if again:
            halo.begin()

    def turn(p):
        if again:
            halo.turn(p)

    def shove():
        for right in rights:
            right.start()

    hooks = {
        1: [shove],
        steps - 2: [lambda: drop(0)],
        steps - 1: [lambda: drop(1), lambda: drop(2), last_right.start],
        2 * steps - 1: [renew, lambda: turn(0), lambda: turn(1)],
    }

    def run_hooks(at):
        for hook in hooks.get(at, ()):
            hook()

    every = range(len(streams))
    for t in every:
        scatter_start(t, 0)
    for s in range(steps):
        for t in every:
            scatter_finish(t, s)
            if s < steps - 1:
                scatter_start(t, s + 1)
            else:
                gather_start(t, s)
        run_hooks(s)
    for s in range(steps - 1, -1, -1):
        for t in every:
            copies[t, steps + s].wait_recv()
            if s > 0:
                gather_start(t, s - 1)
        run_hooks(2 * steps - 1 - s)
    for copy in copies.values():
        copy.wait_send()
    for shift in rights + [last_right] + downs:
        shift.leave()
    if again:
        halo.end()


def shape(*dims):
    return jax.ShapeDtypeStruct(dims, jnp.float32)


def on_device(object_field, amplitudes, positions, frame_count, coefficients, probe_modes):
    frames, length = amplitudes.shape[:2]
    mode_count = probe_modes.shape[0]
    planes = 2 * mode_count
    block_height, block_width = object_field.shape[1:]
    scan_count = lax.axis_size("scan")
    col_count = lax.axis_size("col")
    block_corner = jnp.stack(
        [lax.axis_index("scan") * block_height, lax.axis_index("col") * block_width]
    )
    offsets = positions - block_corner[None, :]
    root_total = math.sqrt(frames * scan_count * col_count)
    rows_table, cols_table = make_tables(length)
    modes = probe_modes.reshape(planes, length, length)
    full_height, full_width = block_height + length, block_width + length
    wide = pl.pallas_call(
        functools.partial(halo_kernel, scan_count, col_count),
        name="halo",
        out_shape=shape(2, full_height, full_width),
        in_specs=[VMEM],
        out_specs=VMEM,
        scratch_shapes=[pltpu.SemaphoreType.DMA((5,))] * 2,
        compiler_params=pltpu.CompilerParams(collective_id=ITERS, has_side_effects=True),
    )(object_field)
    for iteration in range(ITERS):
        again = iteration < ITERS - 1
        totals, mode_terms, stashed = pl.pallas_call(
            frames_kernel,
            name="frames",
            out_shape=(
                shape(3, full_height, full_width),
                shape(planes, length, length),
                shape(frames, 2, length, length),
            ),
            in_specs=[SMEM] * 3 + [VMEM] * 5,
            out_specs=(VMEM,) * 3,
            cost_estimate=pl.CostEstimate(flops=2 * 10**9, bytes_accessed=10**7, transcendentals=0),
        )(
            frame_count, offsets, coefficients, wide, amplitudes, modes, rows_table, cols_table,
        )
        steps = scan_count.bit_length() + col_count.bit_length() - 2
        rows = planes * length
        summed, result = pl.pallas_call(
            functools.partial(exchange_kernel, scan_count, col_count, again),
            name="exchange",
            out_shape=(
                shape(rows, length),
                shape(2, full_height, full_width) if again else shape(2, block_height, block_width),
            ),
            in_specs=[VMEM] * 3,
            out_specs=(VMEM,) * 2,
            scratch_shapes=[
                pltpu.VMEM((rows, length), jnp.float32),
                pltpu.VMEM((rows, length), jnp.float32),
                pltpu.VMEM((3, full_height, length), jnp.float32),
                pltpu.VMEM((3, length, block_width), jnp.float32),
                pltpu.VMEM((3, length, block_width), jnp.float32),
                pltpu.SemaphoreType.DMA((4, 2 * steps)),
                pltpu.SemaphoreType.DMA((4, 2 * steps)),
                pltpu.SemaphoreType.DMA((12,)),
                pltpu.SemaphoreType.DMA((12,)),
            ],
            compiler_params=pltpu.CompilerParams(collective_id=iteration, has_side_effects=True),
        )(wide, totals, mode_terms.reshape(rows, length))
        wide = result
        summed = summed.reshape(planes, length, length)
        modes, coefficients = pl.pallas_call(
            lambda *refs: refit_kernel(root_total, *refs),
            name="refit",
            out_shape=(shape(planes, length, length), shape(frames, mode_count)),
            in_specs=[SMEM] * 2 + [VMEM] * 3,
            out_specs=(VMEM,) * 2,
            scratch_shapes=[pltpu.VMEM((planes, length, length), jnp.float32)],
        )(frame_count, coefficients, summed, modes, stashed)
    return (wide, modes.reshape(probe_modes.shape), coefficients)


def solution(mesh):
    placed = (
        P(None, "scan", "col"),
        P(("scan", "col"), None, None),
        P(("scan", "col"), None),
        P(("scan", "col")),
        P(("scan", "col"), None),
        P(),
    )
    return jax.shard_map(
        on_device,
        mesh=mesh,
        in_specs=placed,
        out_specs=(P(None, "scan", "col"), P(), P(("scan", "col"), None)),
        check_vma=False,
    )
```
